32 devices in a mesh: member: 4 (over y, x), region: 8 (over z, core).
Axes of the slice: x: 2, y: 2, z: 4, core: 2. Of those that a mesh axis runs over, the one named last changes fastest.
Arguments:
- states: float32 [256, 49152], P('member', 'region'), may hold values from -6 to 6
- weights: float32 [256, 49152], P('member', 'region'), may hold values from -6 to 6
- obs_count: int32 [384], P('region'), may hold values from 0 to 32
- neighbours: int32 [384, 12], P('region'), may hold values from 0 to 383, as said below
Outputs:
- increments: float32 [256, 49152], P('member', 'region')
The draws below stay inside these ranges and needn't reach their ends.
Inputs may be any that keep to these rules, and one draw needn't show every extreme that they name: `neighbours`: each row lists 12 distinct tiles, all within 8 tiles of its own tile counting cyclically over the 384 tiles; the list always holds the tile itself and the tiles exactly 8 before and after it, in a drawn order.
All inputs are finite; a program needn't handle non-finite values.
Results may differ from the reference program's by a relative error of at most 0.0003.
Values sent between devices are 32-bit elements; how exact they have to be, the bound alone decides.
A program may use at most 128 MiB of HBM per device.

```python
import jax
import jax.numpy as jnp
from jax import lax

M = 256
TILE = 128
NEIGHBOURS = 12
HALO_TILES = 8
TPD = 12
TILES = 384
ROWS = 49152


def draw_neighbours(key, part):
    spread = jnp.concatenate([jnp.arange(-HALO_TILES + 1, 0, dtype=jnp.int32), jnp.arange(1, HALO_TILES, dtype=jnp.int32)])
    fixed_part = jnp.array([0, -HALO_TILES, HALO_TILES], dtype=jnp.int32)
    picks = NEIGHBOURS - 3
    keys = jax.random.split(jax.random.fold_in(key, 7), TILES)

    def one_tile(tile_key):
        first_key, second_key = jax.random.split(tile_key)
        chosen = spread[jax.random.permutation(first_key, spread.shape[0])[:picks]]
        offsets = jnp.concatenate([fixed_part, chosen])
        return offsets[jax.random.permutation(second_key, NEIGHBOURS)]
    offsets = jax.vmap(one_tile)(keys)
    tiles_here = jnp.arange(TILES, dtype=jnp.int32)[:, None]
    return ((tiles_here + offsets) % TILES).astype(jnp.int32)


def place_ends(values, key, low, high):
    spot = [jax.random.randint(jax.random.fold_in(key, axis), (), 0, length) for axis, length in enumerate(values.shape)]
    longest = values.shape.index(max(values.shape))
    next_to = spot[:longest] + [(spot[longest] + 1) % values.shape[longest]] + spot[longest + 1:]
    return values.at[tuple(spot)].set(low).at[tuple(next_to)].set(high)


def level_of(own_key, dims, shards, low, top_value):
    loudness, own = 1.0, jax.random.fold_in(own_key, 6)
    for dim, shards_of in shards:
        steps = jnp.exp(jax.random.uniform(jax.random.fold_in(own, dim), (shards_of,), jnp.float32, low / len(shards), top_value / len(shards)))
        loudness = loudness * jnp.repeat(steps, dims[dim] // shards_of).reshape([-1 if axis == dim else 1 for axis in range(len(dims))])
    return loudness


def bell_draw(stream_key, extent, deviation, reach, cuts=(), kind=jnp.bfloat16):
    loudness = level_of(stream_key, extent, cuts, -0.22, 0.18) if cuts else 1.0
    drawn = jax.random.normal(stream_key, extent, jnp.float32) * deviation * loudness
    return jnp.minimum(jnp.maximum(drawn, -reach), reach).astype(kind)


def setup_inputs(seed: int = 0) -> dict:
    splits = jax.random.split(jax.random.key(seed), 5)
    states = bell_draw(splits[0], (M, ROWS), 1.0, 6.0, ((0, 4), (1, 8)), jnp.float32)
    weights = bell_draw(splits[1], (M, ROWS), 1.0, 6.0, ((0, 4), (1, 8)), jnp.float32)
    obs_count = place_ends(jax.random.randint(splits[2], (TILES,), 0, 33), jax.random.fold_in(splits[2], 1), 0, 32).astype(jnp.int32)
    neighbours = draw_neighbours(jax.random.fold_in(splits[4], 71), 0)
    return {"states": states, "weights": weights, "obs_count": obs_count, "neighbours": neighbours}


def taper(offset, tile):
    rows = jnp.arange(tile, dtype=jnp.float32)
    spread = tile * offset[:, None, None] + rows[None, None, :] - rows[None, :, None]
    scaled = spread / (2.0 * tile)
    return 1.0 / (1.0 + scaled * scaled)


def reference(states, weights, obs_count, neighbours):
    members = states.shape[0]
    counts = obs_count.astype(jnp.float32)
    factor = counts / (counts + 8.0)
    state_rows = states.T
    weight_rows = weights.T
    anomaly = state_rows - jnp.mean(state_rows, axis=1, keepdims=True)
    scaled = weight_rows.reshape(TILES, TILE, members) * factor[:, None, None]
    blocks = anomaly.reshape(TILES, TILE, members)

    def group(first):
        own = first + jnp.arange(TPD, dtype=jnp.int32)
        mine = lax.dynamic_slice_in_dim(blocks, first, TPD, 0)
        lists = lax.dynamic_slice_in_dim(neighbours, first, TPD, 0)
        total = jnp.zeros((TPD, TILE, members), jnp.float32)
        for slot in range(NEIGHBOURS):
            chosen = lists[:, slot].astype(jnp.int32)
            offset = ((chosen - own + TILES // 2) % TILES - TILES // 2).astype(jnp.float32)
            others = blocks[chosen]
            other_weights = scaled[chosen]
            covar = jnp.einsum("tim,tjm->tij", mine, others, precision=lax.Precision.HIGHEST) / (members - 1.0)
            total = total + jnp.einsum("tij,tjm->tim", taper(offset, TILE) * covar, other_weights, precision=lax.Precision.HIGHEST)
        return total

    starts = jnp.arange(TILES // TPD, dtype=jnp.int32) * TPD
    result = lax.map(group, starts)
    return result.reshape(ROWS, members).T
```

```python
import jax
import jax.numpy as jnp
from jax import lax
from jax.experimental import pallas as pl
from jax.experimental.pallas import tpu as pltpu
from jax.sharding import PartitionSpec as P

TILE = 128
HALO_TILES = 8
TPD = 12


def extended_2(block, sides, width):
    for axis, dim in sides:
        count = lax.axis_size(axis)
        forward = [(i, i + 1) for i in range(count - 1)]
        forward.append((count - 1, 0))
        backward = [(target, source) for source, target in forward]
        low = lax.ppermute(
            lax.slice_in_dim(block, block.shape[dim] - width, None, axis=dim), axis, forward
        )
        high = lax.ppermute(lax.slice_in_dim(block, 0, width, axis=dim), axis, backward)
        block = jnp.concatenate([low, block, high], axis=dim)
    return block


def taper(offset, tile):
    rows = jnp.arange(tile, dtype=jnp.float32)
    spread = tile * offset[:, None, None] + rows[None, None, :] - rows[None, :, None]
    scaled = spread / (2.0 * tile)
    return 1.0 / (1.0 + scaled * scaled)


def shards(states, weights, obs_count, neighbours):
    member_count = lax.axis_size("member")
    region_count = lax.axis_size("region")
    member_part, local_rows = states.shape
    local_tiles = local_rows // TILE
    counts = obs_count.astype(jnp.float32)
    factor = counts / (counts + 8.0)
    scaled = (weights.reshape(member_part, local_tiles, TILE) * factor[None, :, None]).reshape(
        member_part, local_rows
    )
    stacked = jnp.stack([states, scaled])
    rim = HALO_TILES * TILE
    block = TPD * TILE
    padded = extended_2(stacked, (("region", 2),), rim)
    own_block = lax.all_to_all(stacked, "member", split_axis=2, concat_axis=1, tiled=True)
    extended = extended_2(own_block, (("member", 2),), rim)
    below, above = (
        lax.all_gather(padded[:, :, :rim], "member", axis=1, tiled=True),
        lax.all_gather(padded[:, :, rim + local_rows :], "member", axis=1, tiled=True),
    )
    position = lax.axis_index("member")
    lower = jnp.where(position == 0, below, extended[:, :, :rim])
    upper = jnp.where(position == member_count - 1, above, extended[:, :, rim + block :])
    window = jnp.concatenate([lower, extended[:, :, rim : rim + block], upper], axis=2)
    members = window.shape[1]
    anomaly = window[0] - jnp.mean(window[0], axis=0, keepdims=True)
    window_weights = window[1]
    tiles_all = TPD * member_count * region_count
    first_tile = (lax.axis_index("region") * member_count + lax.axis_index("member")) * TPD
    lists = lax.dynamic_slice_in_dim(neighbours, lax.axis_index("member") * TPD, TPD, 0)
    local_ids = (lists - first_tile + HALO_TILES) % tiles_all
    span_count = 2 * HALO_TILES + 1
    tile_places = jnp.arange(TPD, dtype=jnp.int32)
    shift_places = jnp.arange(span_count, dtype=jnp.int32)
    wanted = tile_places[:, None, None] + shift_places[None, None, :]
    keep_table = jnp.sum((local_ids[:, :, None] == wanted).astype(jnp.float32), axis=1)
    mine = anomaly[:, rim : rim + block].reshape(members, TPD, TILE)

    def add_offset(shift, total):
        others = lax.dynamic_slice_in_dim(anomaly, shift * TILE, block, 1).reshape(
            members, TPD, TILE
        )
        other_weights = lax.dynamic_slice_in_dim(window_weights, shift * TILE, block, 1).reshape(
            members, TPD, TILE
        )
        covar = jnp.einsum("mti,mtj->tij", mine, others, precision=lax.Precision.HIGHEST) / (
            members - 1.0
        )
        offset = jnp.full((TPD,), shift - HALO_TILES).astype(jnp.float32)
        keep = lax.dynamic_index_in_dim(keep_table, shift, 1, keepdims=False)
        coefficient = taper(offset, TILE) * covar * keep[:, None, None]
        return total + jnp.einsum(
            "mtj,tij->mti", other_weights, coefficient, precision=lax.Precision.HIGHEST
        )

    total = lax.fori_loop(0, span_count, add_offset, jnp.zeros((members, TPD, TILE), jnp.float32))
    returned = lax.all_to_all(
        total.reshape(members, block), "member", split_axis=0, concat_axis=1, tiled=True
    )
    return returned


BLOCK = 2 * TILE
SPAN = HALO_TILES + 1
RIM = HALO_TILES * TILE
CHUNK = RIM // 2
REACH = HALO_TILES // 2


def split(value):
    high = value.astype(jnp.bfloat16)
    return high, (value - high.astype(jnp.float32)).astype(jnp.bfloat16)


def dot(left, right):
    return jnp.dot(left, right, preferred_element_type=jnp.float32)


def fill_taper(taper_ref, members):
    rows = lax.broadcasted_iota(jnp.int32, (BLOCK, BLOCK), 0)
    columns = lax.broadcasted_iota(jnp.int32, (BLOCK, BLOCK), 1)
    for k in range(SPAN):
        spread = (rows - columns + (2 * k - HALO_TILES) * TILE).astype(jnp.float32) / (2.0 * TILE)
        taper_ref[k] = 1.0 / ((1.0 + spread * spread) * (members - 1.0))


def keep_table_of(neighbours, tiles_all):
    local_tiles = neighbours.shape[0]
    first = lax.axis_index("region") * local_tiles
    own = first + jnp.arange(local_tiles, dtype=jnp.int32)
    shift = (neighbours - own[:, None] + HALO_TILES + 1) % tiles_all
    places = jnp.arange(2 * SPAN + 2, dtype=jnp.int32)
    return jnp.sum((shift[:, :, None] == places).astype(jnp.float32), axis=1)


def region_kernel(
    own_ref, weights_ref, factor_ref, keep_ref, out_ref,
    low_ref, high_ref, low_t_ref, high_t_ref, pair_ref, taper_ref, xh_a, xl_a, xh_b, xl_b,
    held, weight_held, weight_rim, factor_rim,
    own_sem, weight_sem, direct_send, direct_recv, relay_send, relay_recv, rim_send, rim_recv,
):
    part, rows = own_ref.shape
    count = rows // CHUNK
    half = part // 2
    pairs = rows // BLOCK
    member, region = lax.axis_index("member"), lax.axis_index("region")
    regions = lax.axis_size("region")
    beside = member + 1 - 2 * lax.rem(member, 2)
    across = lax.rem(member + 2, 4)
    partners = ((beside, region), (across, region))
    above = (member, lax.rem(region + 1, regions))
    below = (member, lax.rem(region + regions - 1, regions))
    order = (0, count - 1, 1, count - 2)
    early = len(order)

    barrier = pltpu.get_barrier_semaphore()
    for device in partners + (above, below):
        pl.semaphore_signal(barrier, inc=1, device_id=device, device_id_type=pl.DeviceIdType.MESH)
    pl.semaphore_wait(barrier, 4)

    def chunk_at(step):
        return order[step] if isinstance(step, int) and step < early else step - 2

    def copy(source, target, send, recv, device):
        return pltpu.make_async_remote_copy(
            src_ref=source, dst_ref=target, send_sem=send, recv_sem=recv,
            device_id=device, device_id_type=pl.DeviceIdType.MESH,
        )

    def columns_of(chunk):
        return pl.ds(pl.multiple_of(chunk * CHUNK, CHUNK), CHUNK)

    def strip(slot):
        return pl.ds(slot * part, part)

    def own_copy(chunk):
        return pltpu.make_async_copy(
            own_ref.at[:, columns_of(chunk)], held.at[chunk + 2, strip(0)], own_sem.at[chunk]
        )

    def direct(step, side):
        chunk = chunk_at(step)
        return copy(
            own_ref.at[:, columns_of(chunk)], held.at[chunk + 2, strip(1 + side)],
            direct_send.at[side, step], direct_recv.at[side, step], partners[side],
        )

    def relay(step, side):
        chunk = chunk_at(step)
        source, target = pl.ds((2 - side) * part + side * half, half), pl.ds(3 * part + side * half, half)
        return copy(
            held.at[chunk + 2, source], held.at[chunk + 2, target],
            relay_send.at[side, step], relay_recv.at[side, step], partners[side],
        )

    def rim(up, item):
        device = above if up else below
        spot = 0 if up else 1
        if item >= 8:
            edge = slice(rows - RIM, rows) if up else slice(0, RIM)
            source, target = ((weights_ref, weight_rim), (factor_ref, factor_rim))[item - 8]
            source, target = source.at[:, edge], target.at[spot]
        else:
            slot, edge = item // 2, item % 2
            chunk, place = (count - 2 + edge, edge) if up else (edge, count + 2 + edge)
            source = held.at[chunk + 2, strip(slot)] if slot else own_ref.at[:, columns_of(chunk)]
            target = held.at[place, strip(slot)]
        return copy(source, target, rim_send.at[spot, item], rim_recv.at[spot, item], device)

    def rim_of(step, slot):
        chunk = order[step]
        up = chunk >= count - 2
        return rim(up, 2 * slot + (chunk - count + 2 if up else chunk))

    for step in range(3):
        for side in range(2):
            direct(step, side).start()
    for item in (0, 1, 8, 9):
        for up in (True, False):
            rim(up, item).start()
    for chunk in range(count):
        own_copy(chunk).start()
    weight_copy = pltpu.make_async_copy(weights_ref, weight_held, weight_sem)
    weight_copy.start()

    fill_taper(taper_ref, part * 4)

    def prepare_weights(value, columns):
        high, low = split(value)
        pair_ref[0:part, columns] = high
        pair_ref[part : 2 * part, columns] = low

    weight_copy.wait()

    @pl.loop(0, pairs)
    def _(block):
        columns = pl.ds(pl.multiple_of(block * BLOCK, BLOCK), BLOCK)
        target = pl.ds(pl.multiple_of(block * BLOCK + RIM, BLOCK), BLOCK)
        prepare_weights(weight_held[:, columns] * factor_ref[0:1, columns], target)

    def prepare(place, own):
        for b in range(CHUNK // BLOCK):
            value = held[place, :, b * BLOCK : (b + 1) * BLOCK]
            anomaly = value - jnp.mean(value, axis=0, keepdims=True)
            block = place * (CHUNK // BLOCK) + b
            high_t_ref[block], low_t_ref[block] = split(anomaly.T)
            if own:
                high_ref[block - REACH], low_ref[block - REACH] = split(anomaly)

    def work(items, held_x, fresh):
        xh_ref, xl_ref = held_x
        for buffer, (pair, ks) in enumerate(items):
            right_high, right_low = high_ref[pair], low_ref[pair]
            for spot, k in enumerate(ks):
                left_high, left_low = high_t_ref[pair + k], low_t_ref[pair + k]
                covar = dot(left_high, right_high) + dot(left_low, right_high) + dot(left_high, right_low)
                scaled = covar * taper_ref[k]
                for t in range(2):
                    for s in range(2):
                        inner, outer = slice(t * TILE, (t + 1) * TILE), slice(s * TILE, (s + 1) * TILE)
                        value = scaled[inner, outer] * keep_ref[2 * pair + s, 2 * k + t + 1 - s]
                        place = slice(spot * BLOCK + t * TILE, spot * BLOCK + (t + 1) * TILE)
                        xh_ref[buffer, place, outer], xl_ref[buffer, place, outer] = split(value)
        for buffer, (pair, ks) in enumerate(items):
            depth = len(ks) * BLOCK
            columns = pl.ds(pl.multiple_of((pair + ks[0]) * BLOCK, BLOCK), depth)
            both = dot(pair_ref[:, columns], xh_ref[buffer, :depth])
            rest = dot(pair_ref[0:part, columns], xl_ref[buffer, :depth])
            term = both[:part] + both[part:] + rest
            target = pl.ds(pl.multiple_of(pair * BLOCK, BLOCK), BLOCK)
            out_ref[:, target] = term if fresh else out_ref[:, target] + term

    wide, narrow = (xh_a, xl_a), (xh_b, xl_b)

    def ks_of(first, last):
        return tuple(range(first, last + 1))

    def work_edge(base):
        work([(base + i, ks_of(4 - i, 7 - i)) for i in range(4)], narrow, True)

    def work_inner(chunk):
        base = 2 * chunk
        work([(base, ks_of(0, 5)), (base + 1, ks_of(0, 4))], wide, True)
        work([(base - 4 + i, ks_of(8 - i, min(9 - i, 8))) for i in range(4)], narrow, False)

    def work_rim(up):
        place = count + 2 if up else 0
        spot = 1 if up else 0
        for item in range(10):
            rim(not up, item).wait_recv()

        @pl.loop(0, 2)
        def _(edge):
            prepare(place + edge, False)

        for b in range(RIM // BLOCK):
            inner = slice(b * BLOCK, (b + 1) * BLOCK)
            target = slice((rows if up else -RIM) + RIM + b * BLOCK, (rows if up else -RIM) + RIM + (b + 1) * BLOCK)
            prepare_weights(weight_rim[spot, :, inner] * factor_rim[spot, 0:1, inner], target)
        if up:
            work([(pairs - 4 + i, ks_of(8 - i, 8)) for i in range(4)], narrow, False)
        else:
            work([(i, ks_of(0, 3 - i)) for i in range(4)], narrow, False)

    def forward(step):
        for side in range(2):
            direct(step, side).wait_recv()
        for side in range(2):
            relay(step, side).start()
        if isinstance(step, int) and step < early:
            for slot in (1, 2):
                rim_of(step, slot).start()

    for chunk in range(count):
        own_copy(chunk).wait()
    forward(0)

    for step in range(early):
        forward(step + 1)
        for side in range(2):
            direct(step + 3, side).start()
        for side in range(2):
            relay(step, side).wait_recv()
        rim_of(step, 3).start()
        prepare(order[step] + 2, True)
        if step >= 2:
            work_edge(0 if step == 2 else pairs - 4)

    @pl.loop(early, count)
    def _(step):
        @pl.when(step + 1 < count)
        def _():
            forward(step + 1)

        @pl.when(step + 3 < count)
        def _():
            for side in range(2):
                direct(step + 3, side).start()

        for side in range(2):
            relay(step, side).wait_recv()
        chunk = chunk_at(step)
        prepare(chunk + 2, True)
        work_inner(chunk)

        @pl.when(chunk == 5)
        def _():
            work_rim(False)

        @pl.when(chunk == 6)
        def _():
            work_rim(True)

        @pl.when(chunk == count - 4)
        def _():
            base = pairs - 8
            work([(base, (8,)), (base + 1, (7, 8)), (base + 4, (0, 1)), (base + 5, (0,))], narrow, False)

    base = pairs - 6
    work([(base, (6, 7, 8)), (base + 1, (5, 6, 7, 8)), (base + 2, (2, 3)), (base + 3, (1, 2))], narrow, False)
    work([(base + 4, (0, 1)), (base + 5, (0,))], wide, False)

    def sent(step):
        for side in range(2):
            direct(step, side).wait_send()
            relay(step, side).wait_send()

    for step in range(early):
        sent(step)

    @pl.loop(early, count)
    def _(step):
        sent(step)

    for up in (True, False):
        for item in range(10):
            rim(up, item).wait_send()


def region_shards(states, weights, obs_count, neighbours):
    region_count = lax.axis_size("region")
    part, local_rows = states.shape
    members = part * lax.axis_size("member")
    count = local_rows // CHUNK
    pairs = local_rows // BLOCK
    blocks = pairs + 2 * REACH
    counts = obs_count.astype(jnp.float32)
    factor = counts / (counts + 8.0)
    factor_rows = jnp.broadcast_to(factor[None, :, None], (8, local_rows // TILE, TILE)).reshape(8, local_rows)
    keep = keep_table_of(neighbours, region_count * (local_rows // TILE))
    vmem = pl.BlockSpec(memory_space=pltpu.VMEM)
    anywhere = pl.BlockSpec(memory_space=pltpu.HBM)
    dma = pltpu.SemaphoreType.DMA
    bf16, f32 = jnp.bfloat16, jnp.float32
    return pl.pallas_call(
        region_kernel,
        out_shape=jax.ShapeDtypeStruct((part, local_rows), f32),
        in_specs=[anywhere, anywhere, vmem, pl.BlockSpec(memory_space=pltpu.SMEM)],
        out_specs=vmem,
        scratch_shapes=[
            pltpu.VMEM((pairs, members, BLOCK), bf16),
            pltpu.VMEM((pairs, members, BLOCK), bf16),
            pltpu.VMEM((blocks, BLOCK, members), bf16),
            pltpu.VMEM((blocks, BLOCK, members), bf16),
            pltpu.VMEM((2 * part, blocks * BLOCK), bf16),
            pltpu.VMEM((SPAN, BLOCK, BLOCK), f32),
            pltpu.VMEM((2, 6 * BLOCK, BLOCK), bf16),
            pltpu.VMEM((2, 6 * BLOCK, BLOCK), bf16),
            pltpu.VMEM((4, 4 * BLOCK, BLOCK), bf16),
            pltpu.VMEM((4, 4 * BLOCK, BLOCK), bf16),
            pltpu.VMEM((count + 4, members, CHUNK), f32),
            pltpu.VMEM((part, local_rows), f32),
            pltpu.VMEM((2, part, RIM), f32),
            pltpu.VMEM((2, 8, RIM), f32),
            dma((count,)), dma,
            dma((2, count)), dma((2, count)), dma((2, count)), dma((2, count)),
            dma((2, 10)), dma((2, 10)),
        ],
        compiler_params=pltpu.CompilerParams(
            collective_id=0, has_side_effects=True, vmem_limit_bytes=52 * 1024 * 1024
        ),
    )(states, weights, factor_rows, keep)


def fits(states, weights, obs_count, neighbours):
    part, local_rows = states.shape
    members = part * lax.axis_size("member")
    window = local_rows + 2 * RIM
    return (
        lax.axis_size("member") == 4
        and lax.axis_size("region") > 2
        and local_rows % RIM == 0
        and local_rows >= 5 * RIM
        and members == 256
        and window * (members * 12 + part * 16) <= 46 * 1024 * 1024
    )


def either(*arguments):
    return region_shards(*arguments) if fits(*arguments) else shards(*arguments)


def solution(mesh):
    placed = (P("member", "region"), P("member", "region"), P("region"), P("region", None))
    return jax.shard_map(
        either, mesh=mesh, in_specs=placed, out_specs=P("member", "region"), check_vma=False
    )
```

```python
import jax
import jax.numpy as jnp
from jax import lax
from jax.experimental import pallas as pl
from jax.experimental.pallas import tpu as pltpu
from jax.sharding import PartitionSpec as P

TILE = 128
HALO_TILES = 8
TPD = 12


def extended_2(block, sides, width):
    for axis, dim in sides:
        count = lax.axis_size(axis)
        forward = [(i, i + 1) for i in range(count - 1)]
        forward.append((count - 1, 0))
        backward = [(target, source) for source, target in forward]
        low = lax.ppermute(
            lax.slice_in_dim(block, block.shape[dim] - width, None, axis=dim), axis, forward
        )
        high = lax.ppermute(lax.slice_in_dim(block, 0, width, axis=dim), axis, backward)
        block = jnp.concatenate([low, block, high], axis=dim)
    return block


def taper(offset, tile):
    rows = jnp.arange(tile, dtype=jnp.float32)
    spread = tile * offset[:, None, None] + rows[None, None, :] - rows[None, :, None]
    scaled = spread / (2.0 * tile)
    return 1.0 / (1.0 + scaled * scaled)


def shards(states, weights, obs_count, neighbours):
    member_count = lax.axis_size("member")
    region_count = lax.axis_size("region")
    member_part, local_rows = states.shape
    local_tiles = local_rows // TILE
    counts = obs_count.astype(jnp.float32)
    factor = counts / (counts + 8.0)
    scaled = (weights.reshape(member_part, local_tiles, TILE) * factor[None, :, None]).reshape(
        member_part, local_rows
    )
    stacked = jnp.stack([states, scaled])
    rim = HALO_TILES * TILE
    block = TPD * TILE
    padded = extended_2(stacked, (("region", 2),), rim)
    own_block = lax.all_to_all(stacked, "member", split_axis=2, concat_axis=1, tiled=True)
    extended = extended_2(own_block, (("member", 2),), rim)
    below, above = (
        lax.all_gather(padded[:, :, :rim], "member", axis=1, tiled=True),
        lax.all_gather(padded[:, :, rim + local_rows :], "member", axis=1, tiled=True),
    )
    position = lax.axis_index("member")
    lower = jnp.where(position == 0, below, extended[:, :, :rim])
    upper = jnp.where(position == member_count - 1, above, extended[:, :, rim + block :])
    window = jnp.concatenate([lower, extended[:, :, rim : rim + block], upper], axis=2)
    members = window.shape[1]
    anomaly = window[0] - jnp.mean(window[0], axis=0, keepdims=True)
    window_weights = window[1]
    tiles_all = TPD * member_count * region_count
    first_tile = (lax.axis_index("region") * member_count + lax.axis_index("member")) * TPD
    lists = lax.dynamic_slice_in_dim(neighbours, lax.axis_index("member") * TPD, TPD, 0)
    local_ids = (lists - first_tile + HALO_TILES) % tiles_all
    span_count = 2 * HALO_TILES + 1
    tile_places = jnp.arange(TPD, dtype=jnp.int32)
    shift_places = jnp.arange(span_count, dtype=jnp.int32)
    wanted = tile_places[:, None, None] + shift_places[None, None, :]
    keep_table = jnp.sum((local_ids[:, :, None] == wanted).astype(jnp.float32), axis=1)
    mine = anomaly[:, rim : rim + block].reshape(members, TPD, TILE)

    def add_offset(shift, total):
        others = lax.dynamic_slice_in_dim(anomaly, shift * TILE, block, 1).reshape(
            members, TPD, TILE
        )
        other_weights = lax.dynamic_slice_in_dim(window_weights, shift * TILE, block, 1).reshape(
            members, TPD, TILE
        )
        covar = jnp.einsum("mti,mtj->tij", mine, others, precision=lax.Precision.HIGHEST) / (
            members - 1.0
        )
        offset = jnp.full((TPD,), shift - HALO_TILES).astype(jnp.float32)
        keep = lax.dynamic_index_in_dim(keep_table, shift, 1, keepdims=False)
        coefficient = taper(offset, TILE) * covar * keep[:, None, None]
        return total + jnp.einsum(
            "mtj,tij->mti", other_weights, coefficient, precision=lax.Precision.HIGHEST
        )

    total = lax.fori_loop(0, span_count, add_offset, jnp.zeros((members, TPD, TILE), jnp.float32))
    returned = lax.all_to_all(
        total.reshape(members, block), "member", split_axis=0, concat_axis=1, tiled=True
    )
    return returned


BLOCK = 2 * TILE
SPAN = HALO_TILES + 1
RIM = HALO_TILES * TILE
CHUNK = RIM // 2
REACH = HALO_TILES // 2


def split(value):
    high = value.astype(jnp.bfloat16)
    return high, (value - high.astype(jnp.float32)).astype(jnp.bfloat16)


def dot(left, right):
    return jnp.dot(left, right, preferred_element_type=jnp.float32)


def fill_taper(taper_ref, members):
    rows = lax.broadcasted_iota(jnp.int32, (BLOCK, BLOCK), 0)
    columns = lax.broadcasted_iota(jnp.int32, (BLOCK, BLOCK), 1)
    for k in range(SPAN):
        spread = (rows - columns + (2 * k - HALO_TILES) * TILE).astype(jnp.float32) / (2.0 * TILE)
        taper_ref[k] = 1.0 / ((1.0 + spread * spread) * (members - 1.0))


def region_kernel(
    own_ref, weights_ref, count_ref, lists_ref, out_ref,
    low_ref, high_ref, low_t_ref, high_t_ref, pair_ref, taper_ref, xh_a, xl_a, xh_b, xl_b,
    held, weight_held, weight_rim, counts_held, lists_held, turn_ref, factor_ref, keep_ref,
    own_sem, weight_sem, direct_send, direct_recv, relay_send, relay_recv, rim_send, rim_recv, up_sem, down_sem,
):
    part, rows = own_ref.shape
    count = rows // CHUNK
    half = part // 2
    pairs = rows // BLOCK
    tiles = rows // TILE
    rim_tiles = RIM // TILE
    member, region = lax.axis_index("member"), lax.axis_index("region")
    regions = lax.axis_size("region")
    beside = member + 1 - 2 * lax.rem(member, 2)
    across = lax.rem(member + 2, 4)
    partners = ((beside, region), (across, region))
    above = (member, lax.rem(region + 1, regions))
    below = (member, lax.rem(region + regions - 1, regions))
    order = (0, count - 1, 1, count - 2)
    early = len(order)

    first, last = region == 0, region == regions - 1

    def signal(semaphore, device):
        pl.semaphore_signal(semaphore, inc=1, device_id=device, device_id_type=pl.DeviceIdType.MESH)

    barrier = pltpu.get_barrier_semaphore()
    for device in partners:
        signal(barrier, device)

    @pl.when(jnp.logical_not(last))
    def _():
        signal(barrier, above)

    @pl.when(jnp.logical_not(first))
    def _():
        signal(barrier, below)

    @pl.when(first | last)
    def _():
        pl.semaphore_wait(barrier, 3)

    @pl.when(jnp.logical_not(first | last))
    def _():
        pl.semaphore_wait(barrier, 4)

    def chunk_at(step):
        return order[step] if isinstance(step, int) and step < early else step - 2

    def copy(source, target, send, recv, device):
        return pltpu.make_async_remote_copy(
            src_ref=source, dst_ref=target, send_sem=send, recv_sem=recv,
            device_id=device, device_id_type=pl.DeviceIdType.MESH,
        )

    def columns_of(chunk):
        return pl.ds(pl.multiple_of(chunk * CHUNK, CHUNK), CHUNK)

    def piece(step):
        if isinstance(step, int) and step >= count - 1:
            inner = pl.ds((step - count + 1) * BLOCK, BLOCK)
            return count - 3, inner, pl.ds((count - 3) * CHUNK + (step - count + 1) * BLOCK, BLOCK)
        chunk = chunk_at(step)
        return chunk, slice(None), columns_of(chunk)

    def strip(slot):
        return pl.ds(slot * part, part)

    def own_copy(chunk):
        return pltpu.make_async_copy(
            own_ref.at[:, columns_of(chunk)], held.at[chunk + 2, strip(0)], own_sem.at[chunk]
        )

    def direct(step, side):
        chunk, inner, columns = piece(step)
        return copy(
            own_ref.at[:, columns], held.at[chunk + 2, strip(1 + side), inner],
            direct_send.at[side, step], direct_recv.at[side, step], partners[side],
        )

    def relay(step, side):
        chunk, inner, _ = piece(step)
        source, target = pl.ds((2 - side) * part + side * half, half), pl.ds(3 * part + side * half, half)
        return copy(
            held.at[chunk + 2, source, inner], held.at[chunk + 2, target, inner],
            relay_send.at[side, step], relay_recv.at[side, step], partners[side],
        )

    def rim(up, item):
        device = above if up else below
        spot = 0 if up else 1
        if item >= 8:
            edge = slice(rows - RIM, rows) if up else slice(0, RIM)
            if item == 8:
                source, target = weights_ref.at[:, edge], weight_rim.at[spot]
            else:
                source, target = count_ref, counts_held.at[1 + spot]
        else:
            slot, edge = item // 2, item % 2
            chunk, place = (count - 2 + edge, edge) if up else (edge, count + 2 + edge)
            source = held.at[chunk + 2, strip(slot)] if slot else own_ref.at[:, columns_of(chunk)]
            target = held.at[place, strip(slot)]
        return copy(source, target, rim_send.at[spot, item], rim_recv.at[spot, item], device)

    def rim_of(step, slot):
        chunk = order[step]
        up = chunk >= count - 2
        return rim(up, 2 * slot + (chunk - count + 2 if up else chunk))

    for step in range(3):
        for side in range(2):
            direct(step, side).start()
    count_copy = pltpu.make_async_copy(count_ref, counts_held.at[0], weight_sem.at[1])
    lists_copy = pltpu.make_async_copy(lists_ref, lists_held, weight_sem.at[2])
    weight_copy = pltpu.make_async_copy(weights_ref, weight_held, weight_sem.at[0])
    count_copy.start()
    lists_copy.start()
    weight_copy.start()
    for chunk in range(count):
        own_copy(chunk).start()

    fill_taper(taper_ref, part * 4)
    turn_ref[...] = jnp.zeros_like(turn_ref)

    @pl.when(first)
    def _():
        signal(up_sem, above)
        pl.semaphore_wait(down_sem, 1)

    @pl.when(last)
    def _():
        signal(down_sem, below)
        pl.semaphore_wait(up_sem, 1)

    @pl.when(jnp.logical_not(first | last))
    def _():
        pl.semaphore_wait(up_sem, 1)
        signal(up_sem, above)
        pl.semaphore_wait(down_sem, 1)
        signal(down_sem, below)

    for item in (0, 1, 9, 8):
        for up in (True, False):
            rim(up, item).start()

    def prepare_weights(value, columns):
        high, low = split(value)
        pair_ref[0:part, columns] = high
        pair_ref[part : 2 * part, columns] = low

    def factors_of(which):
        turn_ref[0:1, 0:tiles] = counts_held[which].astype(jnp.float32)
        spread = jnp.broadcast_to(turn_ref[...].T[0:tiles, 0:1], (tiles, TILE))
        return spread / (spread + 8.0)

    count_copy.wait()
    factor_ref[...] = factors_of(0)
    lists_copy.wait()
    tiles_all = regions * tiles
    own_tile = region * tiles + lax.broadcasted_iota(jnp.int32, lists_held.shape, 1)
    shift = lists_held[...] - own_tile + HALO_TILES
    shift = jnp.where(shift < 0, shift + tiles_all, jnp.where(shift >= tiles_all, shift - tiles_all, shift))
    turn_ref[0 : shift.shape[0], 0:tiles] = shift.astype(jnp.float32)
    turned = turn_ref[...].T
    spreads = [jnp.broadcast_to(turned[0:tiles, i : i + 1], (tiles, TILE)) for i in range(shift.shape[0])]
    for place in range(2 * HALO_TILES + 3):
        total = jnp.zeros((tiles, TILE), jnp.float32)
        for spread in spreads:
            total = total + jnp.where(spread == place - 1.0, 1.0, 0.0)
        keep_ref[place] = total

    weight_copy.wait()

    @pl.loop(0, pairs)
    def _(block):
        for t in range(2):
            start = block * BLOCK + t * TILE
            columns = pl.ds(pl.multiple_of(start, TILE), TILE)
            target = pl.ds(pl.multiple_of(start + RIM, TILE), TILE)
            prepare_weights(weight_held[:, columns] * factor_ref[pl.ds(2 * block + t, 1)], target)

    def prepare(place, own, parts=(0, 1)):
        for b in parts:
            value = held[place, :, b * BLOCK : (b + 1) * BLOCK]
            anomaly = value - jnp.mean(value, axis=0, keepdims=True)
            block = place * (CHUNK // BLOCK) + b
            high_t_ref[block], low_t_ref[block] = split(anomaly.T)
            if own:
                high_ref[block - REACH], low_ref[block - REACH] = split(anomaly)

    def put(scaled, pair, k, held_x, buffer, spot):
        xh_ref, xl_ref = held_x
        for t in range(2):
            for s in range(2):
                inner, outer = slice(t * TILE, (t + 1) * TILE), slice(s * TILE, (s + 1) * TILE)
                value = scaled[inner, outer] * keep_ref[2 * k + t + 1 - s, pl.ds(2 * pair + s, 1)]
                place = slice(spot * BLOCK + t * TILE, spot * BLOCK + (t + 1) * TILE)
                xh_ref[buffer, place, outer], xl_ref[buffer, place, outer] = split(value)

    def cross(pair, k, place, mirror=None):
        left_high, left_low = high_t_ref[pair + k], low_t_ref[pair + k]
        right_high, right_low = high_ref[pair], low_ref[pair]
        covar = dot(left_high, right_high) + dot(left_low, right_high) + dot(left_high, right_low)
        scaled = covar * taper_ref[k]
        put(scaled, pair, k, *place)
        if mirror is not None:
            put(scaled.T, pair + k - REACH, 2 * REACH - k, *mirror)

    def apply(pair, k, length, held_x, buffer, fresh, spot=0):
        xh_ref, xl_ref = held_x
        columns = pl.ds(pl.multiple_of((pair + k) * BLOCK, BLOCK), length * BLOCK)
        place = slice(spot * BLOCK, (spot + length) * BLOCK)
        both = dot(pair_ref[:, columns], xh_ref[buffer, place])
        term = both[:part] + both[part:] + dot(pair_ref[0:part, columns], xl_ref[buffer, place])
        target = pl.ds(pl.multiple_of(pair * BLOCK, BLOCK), BLOCK)
        out_ref[:, target] = term if fresh else out_ref[:, target] + term

    wide, narrow = (xh_a, xl_a), (xh_b, xl_b)

    def work_edge(base):
        for i in range(4):
            for j in range(i):
                cross(base + i, REACH + j - i, (narrow, i, j), (narrow, j, i))
            cross(base + i, REACH, (narrow, i, i))
        for i in range(4):
            apply(base + i, REACH - i, 4, narrow, i, True)

    def work_inner(chunk):
        base = 2 * chunk
        for i in range(4):
            cross(base, i, (wide, 0, i), (narrow, i, 0))
        cross(base, 4, (wide, 0, 4))
        cross(base, 5, (wide, 0, 5), (wide, 1, 3))
        for i in range(3):
            cross(base + 1, i, (wide, 1, i), (narrow, i + 1, 1))
        cross(base + 1, 4, (wide, 1, 4))
        apply(base, 0, 6, wide, 0, True)
        apply(base + 1, 0, 5, wide, 1, True)
        for i in range(4):
            apply(base - 4 + i, 8 - i, min(i + 1, 2), narrow, i, False)

    def work_close():
        base = pairs - 8
        cross(base, 8, (narrow, 0, 0), (narrow, 2, 0))
        cross(base + 1, 7, (narrow, 1, 0), (narrow, 2, 1))
        cross(base + 1, 8, (narrow, 1, 1), (narrow, 3, 0))
        apply(base, 8, 1, narrow, 0, False)
        apply(base + 1, 7, 2, narrow, 1, False)
        apply(base + 4, 0, 2, narrow, 2, False)
        apply(base + 5, 0, 1, narrow, 3, False)

    def work_last(base, gap):
        above_ks = range(REACH + 1 + gap, 2 * REACH + 1)
        for i in range(REACH):
            cross(base, i, (wide, 0, i), (narrow, i, 0))
        cross(base, REACH, (wide, 0, REACH))
        for i, k in enumerate(above_ks):
            cross(base, k, (wide, 1, i), (narrow, i, 1))
        apply(base, 0, REACH + 1, wide, 0, True)
        apply(base, above_ks[0], len(above_ks), wide, 1, False)
        for i in range(REACH):
            apply(base - REACH + i, 2 * REACH - i, 1, narrow, i, False)
        for i, k in enumerate(above_ks):
            apply(base + k - REACH, 2 * REACH - k, 1, narrow, i, False, 1)

    def work_rim(up):
        place = count + 2 if up else 0
        spot = 1 if up else 0
        for item in range(10):
            rim(not up, item).wait_recv()

        @pl.loop(0, 2)
        def _(edge):
            prepare(place + edge, False)

        factors = factors_of(1 + spot)
        for t in range(rim_tiles):
            inner = slice(t * TILE, (t + 1) * TILE)
            start = (rows + RIM if up else 0) + t * TILE
            tile = t if up else tiles - rim_tiles + t
            prepare_weights(weight_rim[spot, :, inner] * factors[tile : tile + 1], slice(start, start + TILE))
        for i in range(4):
            pair, first_k, length = (pairs - 4 + i, 8 - i, i + 1) if up else (i, 0, 4 - i)
            for spot in range(length):
                cross(pair, first_k + spot, (narrow, i, spot))
        for i in range(4):
            pair, first_k, length = (pairs - 4 + i, 8 - i, i + 1) if up else (i, 0, 4 - i)
            apply(pair, first_k, length, narrow, i, False)

    def forward(step):
        for side in range(2):
            direct(step, side).wait_recv()
        for side in range(2):
            relay(step, side).start()
        if isinstance(step, int) and step < early:
            for slot in (1, 2):
                rim_of(step, slot).start()

    for chunk in range(count):
        own_copy(chunk).wait()
    forward(0)

    for step in range(early):
        forward(step + 1)
        for side in range(2):
            direct(step + 3, side).start()
        for side in range(2):
            relay(step, side).wait_recv()
        rim_of(step, 3).start()
        prepare(order[step] + 2, True)
        if step >= 2:
            work_edge(0 if step == 2 else pairs - 4)

    ends = (count - 1, count)

    @pl.loop(early, count - 1)
    def _(step):
        @pl.when(step + 1 < count - 1)
        def _():
            forward(step + 1)

        @pl.when(step + 3 < count - 1)
        def _():
            for side in range(2):
                direct(step + 3, side).start()

        for end in ends:
            @pl.when(step + 3 == end)
            def _():
                for side in range(2):
                    direct(end, side).start()

            @pl.when(step + 1 == end)
            def _():
                forward(end)

        for side in range(2):
            relay(step, side).wait_recv()
        chunk = chunk_at(step)
        prepare(chunk + 2, True)
        work_inner(chunk)

        @pl.when(chunk == 4)
        def _():
            work_rim(False)

        @pl.when(chunk == 5)
        def _():
            work_rim(True)

        @pl.when(chunk == count - 4)
        def _():
            work_close()

    forward(ends[1])
    for side in range(2):
        relay(ends[0], side).wait_recv()
    prepare(count - 1, True, (0,))
    work_last(pairs - 6, 1)

    for side in range(2):
        relay(ends[1], side).wait_recv()
    prepare(count - 1, True, (1,))
    work_last(pairs - 5, 0)

    def sent(step):
        for side in range(2):
            direct(step, side).wait_send()
            relay(step, side).wait_send()

    for step in tuple(range(early)) + ends:
        sent(step)

    @pl.loop(early, count - 1)
    def _(step):
        sent(step)

    for up in (True, False):
        for item in range(10):
            rim(up, item).wait_send()


def region_shards(states, weights, obs_count, neighbours):
    part, local_rows = states.shape
    members = part * lax.axis_size("member")
    count = local_rows // CHUNK
    pairs = local_rows // BLOCK
    blocks = pairs + 2 * REACH
    tiles, listed = neighbours.shape
    vmem = pl.BlockSpec(memory_space=pltpu.VMEM)
    anywhere = pl.BlockSpec(memory_space=pltpu.HBM)
    dma = pltpu.SemaphoreType.DMA
    bf16, f32 = jnp.bfloat16, jnp.float32
    return pl.pallas_call(
        region_kernel,
        out_shape=jax.ShapeDtypeStruct((part, local_rows), f32),
        in_specs=[anywhere, anywhere, anywhere, anywhere],
        out_specs=vmem,
        scratch_shapes=[
            pltpu.VMEM((pairs, members, BLOCK), bf16),
            pltpu.VMEM((pairs, members, BLOCK), bf16),
            pltpu.VMEM((blocks, BLOCK, members), bf16),
            pltpu.VMEM((blocks, BLOCK, members), bf16),
            pltpu.VMEM((2 * part, blocks * BLOCK), bf16),
            pltpu.VMEM((SPAN, BLOCK, BLOCK), f32),
            pltpu.VMEM((2, 6 * BLOCK, BLOCK), bf16),
            pltpu.VMEM((2, 6 * BLOCK, BLOCK), bf16),
            pltpu.VMEM((4, 4 * BLOCK, BLOCK), bf16),
            pltpu.VMEM((4, 4 * BLOCK, BLOCK), bf16),
            pltpu.VMEM((count + 4, members, CHUNK), f32),
            pltpu.VMEM((part, local_rows), f32),
            pltpu.VMEM((2, part, RIM), f32),
            pltpu.VMEM((3, 1, tiles), jnp.int32),
            pltpu.VMEM((listed, tiles), jnp.int32),
            pltpu.VMEM((TILE, TILE), f32),
            pltpu.VMEM((tiles, TILE), f32),
            pltpu.VMEM((2 * HALO_TILES + 3, tiles, TILE), f32),
            dma((count,)), dma((3,)),
            dma((2, count + 1)), dma((2, count + 1)), dma((2, count + 1)), dma((2, count + 1)),
            dma((2, 10)), dma((2, 10)),
            pltpu.SemaphoreType.REGULAR, pltpu.SemaphoreType.REGULAR,
        ],
        compiler_params=pltpu.CompilerParams(
            collective_id=0, has_side_effects=True, vmem_limit_bytes=52 * 1024 * 1024
        ),
    )(states, weights, obs_count.reshape(1, tiles), neighbours.T)


def fits(states, weights, obs_count, neighbours):
    part, local_rows = states.shape
    members = part * lax.axis_size("member")
    window = local_rows + 2 * RIM
    return (
        lax.axis_size("member") == 4
        and lax.axis_size("region") > 2
        and local_rows % RIM == 0
        and 5 * RIM <= local_rows <= TILE * TILE
        and members == 256
        and window * (members * 12 + part * 16) <= 46 * 1024 * 1024
    )


def either(*arguments):
    return region_shards(*arguments) if fits(*arguments) else shards(*arguments)


def solution(mesh):
    placed = (P("member", "region"), P("member", "region"), P("region"), P("region", None))
    return jax.shard_map(
        either, mesh=mesh, in_specs=placed, out_specs=P("member", "region"), check_vma=False
    )
```

```python
import jax
import jax.numpy as jnp
from jax import lax
from jax.experimental import pallas as pl
from jax.experimental.pallas import tpu as pltpu
from jax.sharding import PartitionSpec as P

TILE = 128
HALO_TILES = 8
TPD = 12


def extended_2(block, sides, width):
    for axis, dim in sides:
        count = lax.axis_size(axis)
        forward = [(i, i + 1) for i in range(count - 1)]
        forward.append((count - 1, 0))
        backward = [(target, source) for source, target in forward]
        low = lax.ppermute(
            lax.slice_in_dim(block, block.shape[dim] - width, None, axis=dim), axis, forward
        )
        high = lax.ppermute(lax.slice_in_dim(block, 0, width, axis=dim), axis, backward)
        block = jnp.concatenate([low, block, high], axis=dim)
    return block


def taper(offset, tile):
    rows = jnp.arange(tile, dtype=jnp.float32)
    spread = tile * offset[:, None, None] + rows[None, None, :] - rows[None, :, None]
    scaled = spread / (2.0 * tile)
    return 1.0 / (1.0 + scaled * scaled)


def shards(states, weights, obs_count, neighbours):
    member_count = lax.axis_size("member")
    region_count = lax.axis_size("region")
    member_part, local_rows = states.shape
    local_tiles = local_rows // TILE
    counts = obs_count.astype(jnp.float32)
    factor = counts / (counts + 8.0)
    scaled = (weights.reshape(member_part, local_tiles, TILE) * factor[None, :, None]).reshape(
        member_part, local_rows
    )
    stacked = jnp.stack([states, scaled])
    rim = HALO_TILES * TILE
    block = TPD * TILE
    padded = extended_2(stacked, (("region", 2),), rim)
    own_block = lax.all_to_all(stacked, "member", split_axis=2, concat_axis=1, tiled=True)
    extended = extended_2(own_block, (("member", 2),), rim)
    below, above = (
        lax.all_gather(padded[:, :, :rim], "member", axis=1, tiled=True),
        lax.all_gather(padded[:, :, rim + local_rows :], "member", axis=1, tiled=True),
    )
    position = lax.axis_index("member")
    lower = jnp.where(position == 0, below, extended[:, :, :rim])
    upper = jnp.where(position == member_count - 1, above, extended[:, :, rim + block :])
    window = jnp.concatenate([lower, extended[:, :, rim : rim + block], upper], axis=2)
    members = window.shape[1]
    anomaly = window[0] - jnp.mean(window[0], axis=0, keepdims=True)
    window_weights = window[1]
    tiles_all = TPD * member_count * region_count
    first_tile = (lax.axis_index("region") * member_count + lax.axis_index("member")) * TPD
    lists = lax.dynamic_slice_in_dim(neighbours, lax.axis_index("member") * TPD, TPD, 0)
    local_ids = (lists - first_tile + HALO_TILES) % tiles_all
    span_count = 2 * HALO_TILES + 1
    tile_places = jnp.arange(TPD, dtype=jnp.int32)
    shift_places = jnp.arange(span_count, dtype=jnp.int32)
    wanted = tile_places[:, None, None] + shift_places[None, None, :]
    keep_table = jnp.sum((local_ids[:, :, None] == wanted).astype(jnp.float32), axis=1)
    mine = anomaly[:, rim : rim + block].reshape(members, TPD, TILE)

    def add_offset(shift, total):
        others = lax.dynamic_slice_in_dim(anomaly, shift * TILE, block, 1).reshape(
            members, TPD, TILE
        )
        other_weights = lax.dynamic_slice_in_dim(window_weights, shift * TILE, block, 1).reshape(
            members, TPD, TILE
        )
        covar = jnp.einsum("mti,mtj->tij", mine, others, precision=lax.Precision.HIGHEST) / (
            members - 1.0
        )
        offset = jnp.full((TPD,), shift - HALO_TILES).astype(jnp.float32)
        keep = lax.dynamic_index_in_dim(keep_table, shift, 1, keepdims=False)
        coefficient = taper(offset, TILE) * covar * keep[:, None, None]
        return total + jnp.einsum(
            "mtj,tij->mti", other_weights, coefficient, precision=lax.Precision.HIGHEST
        )

    total = lax.fori_loop(0, span_count, add_offset, jnp.zeros((members, TPD, TILE), jnp.float32))
    returned = lax.all_to_all(
        total.reshape(members, block), "member", split_axis=0, concat_axis=1, tiled=True
    )
    return returned


BLOCK = 2 * TILE
SPAN = HALO_TILES + 1
RIM = HALO_TILES * TILE
CHUNK = RIM // 2
REACH = HALO_TILES // 2


def split(value):
    high = value.astype(jnp.bfloat16)
    return high, (value - high.astype(jnp.float32)).astype(jnp.bfloat16)


def dot(left, right):
    return jnp.dot(left, right, preferred_element_type=jnp.float32)


def fill_taper(taper_ref, members):
    rows = lax.broadcasted_iota(jnp.int32, (BLOCK, BLOCK), 0)
    columns = lax.broadcasted_iota(jnp.int32, (BLOCK, BLOCK), 1)
    for k in range(SPAN):
        spread = (rows - columns + (2 * k - HALO_TILES) * TILE).astype(jnp.float32) / (2.0 * TILE)
        taper_ref[k] = 1.0 / ((1.0 + spread * spread) * (members - 1.0))


def region_kernel(
    own_ref, weights_ref, count_ref, lists_ref, out_ref,
    low_ref, high_ref, low_t_ref, high_t_ref, pair_ref, taper_ref, xh_a, xl_a, xh_b, xl_b,
    held, weight_held, weight_rim, counts_held, lists_held, turn_ref, factor_ref, keep_ref,
    own_sem, weight_sem, direct_send, direct_recv, relay_send, relay_recv, rim_send, rim_recv, up_sem, down_sem,
):
    part, rows = own_ref.shape
    count = rows // CHUNK
    half = part // 2
    pairs = rows // BLOCK
    tiles = rows // TILE
    rim_tiles = RIM // TILE
    member, region = lax.axis_index("member"), lax.axis_index("region")
    regions = lax.axis_size("region")
    beside = member + 1 - 2 * lax.rem(member, 2)
    across = lax.rem(member + 2, 4)
    partners = ((beside, region), (across, region))
    above = (member, lax.rem(region + 1, regions))
    below = (member, lax.rem(region + regions - 1, regions))
    order = (0, count - 1, 1, count - 2)
    early = len(order)

    first, last = region == 0, region == regions - 1

    def signal(semaphore, device):
        pl.semaphore_signal(semaphore, inc=1, device_id=device, device_id_type=pl.DeviceIdType.MESH)

    barrier = pltpu.get_barrier_semaphore()
    for device in partners:
        signal(barrier, device)

    @pl.when(jnp.logical_not(last))
    def _():
        signal(barrier, above)

    @pl.when(jnp.logical_not(first))
    def _():
        signal(barrier, below)

    @pl.when(first | last)
    def _():
        pl.semaphore_wait(barrier, 3)

    @pl.when(jnp.logical_not(first | last))
    def _():
        pl.semaphore_wait(barrier, 4)

    def chunk_at(step):
        return order[step] if isinstance(step, int) and step < early else step - 2

    def copy(source, target, send, recv, device):
        return pltpu.make_async_remote_copy(
            src_ref=source, dst_ref=target, send_sem=send, recv_sem=recv,
            device_id=device, device_id_type=pl.DeviceIdType.MESH,
        )

    def columns_of(chunk):
        return pl.ds(pl.multiple_of(chunk * CHUNK, CHUNK), CHUNK)

    def piece(step):
        if isinstance(step, int) and step >= count - 1:
            inner = pl.ds((step - count + 1) * BLOCK, BLOCK)
            return count - 3, inner, pl.ds((count - 3) * CHUNK + (step - count + 1) * BLOCK, BLOCK)
        chunk = chunk_at(step)
        return chunk, slice(None), columns_of(chunk)

    def strip(slot):
        return pl.ds(slot * part, part)

    def own_copy(chunk):
        return pltpu.make_async_copy(
            own_ref.at[:, columns_of(chunk)], held.at[chunk + 2, strip(0)], own_sem.at[chunk]
        )

    def direct(step, side):
        chunk, inner, columns = piece(step)
        return copy(
            own_ref.at[:, columns], held.at[chunk + 2, strip(1 + side), inner],
            direct_send.at[side, step], direct_recv.at[side, step], partners[side],
        )

    def relay(step, side):
        chunk, inner, _ = piece(step)
        source, target = pl.ds((2 - side) * part + side * half, half), pl.ds(3 * part + side * half, half)
        return copy(
            held.at[chunk + 2, source, inner], held.at[chunk + 2, target, inner],
            relay_send.at[side, step], relay_recv.at[side, step], partners[side],
        )

    def rim(up, item):
        device = above if up else below
        spot = 0 if up else 1
        if item >= 8:
            edge = slice(rows - RIM, rows) if up else slice(0, RIM)
            if item == 8:
                source, target = weights_ref.at[:, edge], weight_rim.at[spot]
            else:
                source, target = count_ref, counts_held.at[1 + spot]
        else:
            slot, edge = item // 2, item % 2
            chunk, place = (count - 2 + edge, edge) if up else (edge, count + 2 + edge)
            source = held.at[chunk + 2, strip(slot)] if slot else own_ref.at[:, columns_of(chunk)]
            target = held.at[place, strip(slot)]
        return copy(source, target, rim_send.at[spot, item], rim_recv.at[spot, item], device)

    def rim_of(step, slot):
        chunk = order[step]
        up = chunk >= count - 2
        return rim(up, 2 * slot + (chunk - count + 2 if up else chunk))

    for step in range(3):
        for side in range(2):
            direct(step, side).start()
    count_copy = pltpu.make_async_copy(count_ref, counts_held.at[0], weight_sem.at[1])
    lists_copy = pltpu.make_async_copy(lists_ref, lists_held, weight_sem.at[2])
    weight_copy = pltpu.make_async_copy(weights_ref, weight_held, weight_sem.at[0])
    count_copy.start()
    lists_copy.start()
    weight_copy.start()
    for chunk in range(count):
        own_copy(chunk).start()

    fill_taper(taper_ref, part * 4)
    turn_ref[...] = jnp.zeros_like(turn_ref)

    @pl.when(first)
    def _():
        signal(up_sem, above)
        pl.semaphore_wait(down_sem, 1)

    @pl.when(last)
    def _():
        signal(down_sem, below)
        pl.semaphore_wait(up_sem, 1)

    @pl.when(jnp.logical_not(first | last))
    def _():
        pl.semaphore_wait(up_sem, 1)
        signal(up_sem, above)
        pl.semaphore_wait(down_sem, 1)
        signal(down_sem, below)

    for item in (0, 1, 9, 8):
        for up in (True, False):
            rim(up, item).start()

    def prepare_weights(value, columns):
        high, low = split(value)
        pair_ref[0:part, columns] = high
        pair_ref[part : 2 * part, columns] = low

    def factors_of(which):
        turn_ref[0:1, 0:tiles] = counts_held[which].astype(jnp.float32)
        spread = jnp.broadcast_to(turn_ref[...].T[0:tiles, 0:1], (tiles, TILE))
        return spread / (spread + 8.0)

    count_copy.wait()
    factor_ref[...] = factors_of(0)
    lists_copy.wait()
    tiles_all = regions * tiles
    own_tile = region * tiles + lax.broadcasted_iota(jnp.int32, lists_held.shape, 1)
    shift = lists_held[...] - own_tile + HALO_TILES
    shift = jnp.where(shift < 0, shift + tiles_all, jnp.where(shift >= tiles_all, shift - tiles_all, shift))
    turn_ref[0 : shift.shape[0], 0:tiles] = shift.astype(jnp.float32)
    turned = turn_ref[...].T
    spreads = [jnp.broadcast_to(turned[0:tiles, i : i + 1], (tiles, TILE)) for i in range(shift.shape[0])]
    for place in range(2 * HALO_TILES + 3):
        total = jnp.zeros((tiles, TILE), jnp.float32)
        for spread in spreads:
            total = total + jnp.where(spread == place - 1.0, 1.0, 0.0)
        keep_ref[place] = total

    weight_copy.wait()

    @pl.loop(0, pairs)
    def _(block):
        for t in range(2):
            start = block * BLOCK + t * TILE
            columns = pl.ds(pl.multiple_of(start, TILE), TILE)
            target = pl.ds(pl.multiple_of(start + RIM, TILE), TILE)
            prepare_weights(weight_held[:, columns] * factor_ref[pl.ds(2 * block + t, 1)], target)

    def prepare(place, own, parts=(0, 1)):
        for b in parts:
            value = held[place, :, b * BLOCK : (b + 1) * BLOCK]
            anomaly = value - jnp.mean(value, axis=0, keepdims=True)
            block = place * (CHUNK // BLOCK) + b
            high_t_ref[block], low_t_ref[block] = split(anomaly.T)
            if own:
                high_ref[block - REACH], low_ref[block - REACH] = split(anomaly)

    def put(scaled, pair, k, held_x, buffer, spot):
        xh_ref, xl_ref = held_x
        for t in range(2):
            for s in range(2):
                inner, outer = slice(t * TILE, (t + 1) * TILE), slice(s * TILE, (s + 1) * TILE)
                value = scaled[inner, outer] * keep_ref[2 * k + t + 1 - s, pl.ds(2 * pair + s, 1)]
                place = slice(spot * BLOCK + t * TILE, spot * BLOCK + (t + 1) * TILE)
                xh_ref[buffer, place, outer], xl_ref[buffer, place, outer] = split(value)

    def cross(pair, k, place, mirror=None):
        left_high, left_low = high_t_ref[pair + k], low_t_ref[pair + k]
        right_high, right_low = high_ref[pair], low_ref[pair]
        covar = dot(left_high, right_high) + dot(left_low, right_high) + dot(left_high, right_low)
        scaled = covar * taper_ref[k]
        put(scaled, pair, k, *place)
        if mirror is not None:
            put(scaled.T, pair + k - REACH, 2 * REACH - k, *mirror)

    def apply(pair, k, length, held_x, buffer, fresh, spot=0):
        xh_ref, xl_ref = held_x
        columns = pl.ds(pl.multiple_of((pair + k) * BLOCK, BLOCK), length * BLOCK)
        place = slice(spot * BLOCK, (spot + length) * BLOCK)
        both = dot(pair_ref[:, columns], xh_ref[buffer, place])
        term = both[:part] + both[part:] + dot(pair_ref[0:part, columns], xl_ref[buffer, place])
        target = pl.ds(pl.multiple_of(pair * BLOCK, BLOCK), BLOCK)
        out_ref[:, target] = term if fresh else out_ref[:, target] + term

    wide, narrow = (xh_a, xl_a), (xh_b, xl_b)

    def work_edge(base):
        for i in range(4):
            for j in range(i):
                cross(base + i, REACH + j - i, (narrow, i, j), (narrow, j, i))
            cross(base + i, REACH, (narrow, i, i))
        for i in range(4):
            apply(base + i, REACH - i, 4, narrow, i, True)

    def work_inner(chunk):
        base = 2 * chunk
        for i in range(4):
            cross(base, i, (wide, 0, i), (narrow, i, 0))
        cross(base, 4, (wide, 0, 4))
        cross(base, 5, (wide, 0, 5), (wide, 1, 3))
        for i in range(3):
            cross(base + 1, i, (wide, 1, i), (narrow, i + 1, 1))
        cross(base + 1, 4, (wide, 1, 4))
        apply(base, 0, 6, wide, 0, True)
        apply(base + 1, 0, 5, wide, 1, True)
        for i in range(4):
            apply(base - 4 + i, 8 - i, min(i + 1, 2), narrow, i, False)

    def work_close():
        base = pairs - 8
        cross(base, 8, (narrow, 0, 0), (narrow, 2, 0))
        cross(base + 1, 7, (narrow, 1, 0), (narrow, 2, 1))
        cross(base + 1, 8, (narrow, 1, 1), (narrow, 3, 0))
        apply(base, 8, 1, narrow, 0, False)
        apply(base + 1, 7, 2, narrow, 1, False)
        apply(base + 4, 0, 2, narrow, 2, False)
        apply(base + 5, 0, 1, narrow, 3, False)

    def work_last(base, gap):
        above_ks = range(REACH + 1 + gap, 2 * REACH + 1)
        for i in range(REACH):
            cross(base, i, (wide, 0, i), (narrow, i, 0))
        cross(base, REACH, (wide, 0, REACH))
        for i, k in enumerate(above_ks):
            cross(base, k, (wide, 1, i), (narrow, i, 1))
        apply(base, 0, REACH + 1, wide, 0, True)
        apply(base, above_ks[0], len(above_ks), wide, 1, False)
        for i in range(REACH):
            apply(base - REACH + i, 2 * REACH - i, 1, narrow, i, False)
        for i, k in enumerate(above_ks):
            apply(base + k - REACH, 2 * REACH - k, 1, narrow, i, False, 1)

    def work_rim(up):
        place = count + 2 if up else 0
        spot = 1 if up else 0
        for item in range(10):
            rim(not up, item).wait_recv()

        @pl.loop(0, 2)
        def _(edge):
            prepare(place + edge, False)

        factors = factors_of(1 + spot)
        for t in range(rim_tiles):
            inner = slice(t * TILE, (t + 1) * TILE)
            start = (rows + RIM if up else 0) + t * TILE
            tile = t if up else tiles - rim_tiles + t
            prepare_weights(weight_rim[spot, :, inner] * factors[tile : tile + 1], slice(start, start + TILE))
        for i in range(4):
            pair, first_k, length = (pairs - 4 + i, 8 - i, i + 1) if up else (i, 0, 4 - i)
            for spot in range(length):
                cross(pair, first_k + spot, (narrow, i, spot))
        for i in range(4):
            pair, first_k, length = (pairs - 4 + i, 8 - i, i + 1) if up else (i, 0, 4 - i)
            apply(pair, first_k, length, narrow, i, False)

    def forward(step):
        for side in range(2):
            direct(step, side).wait_recv()
        for side in range(2):
            relay(step, side).start()
        if isinstance(step, int) and step < early:
            for slot in (1, 2):
                rim_of(step, slot).start()

    for chunk in range(count):
        own_copy(chunk).wait()
    forward(0)

    for step in range(early):
        forward(step + 1)
        for side in range(2):
            direct(step + 3, side).start()
        for side in range(2):
            relay(step, side).wait_recv()
        rim_of(step, 3).start()
        prepare(order[step] + 2, True)
        if step >= 2:
            work_edge(0 if step == 2 else pairs - 4)

    ends = (count - 1, count)

    @pl.loop(early, count - 1)
    def _(step):
        @pl.when(step + 1 < count - 1)
        def _():
            forward(step + 1)

        @pl.when(step + 3 < count - 1)
        def _():
            for side in range(2):
                direct(step + 3, side).start()

        for end in ends:
            @pl.when(step + 3 == end)
            def _():
                for side in range(2):
                    direct(end, side).start()

            @pl.when(step + 1 == end)
            def _():
                forward(end)

        for side in range(2):
            relay(step, side).wait_recv()
        chunk = chunk_at(step)
        prepare(chunk + 2, True)
        work_inner(chunk)

        @pl.when(chunk == 4)
        def _():
            work_rim(False)

        @pl.when(chunk == 5)
        def _():
            work_rim(True)

        @pl.when(chunk == count - 4)
        def _():
            forward(ends[1])
            work_close()

    for side in range(2):
        relay(ends[0], side).wait_recv()
    prepare(count - 1, True, (0,))
    work_last(pairs - 6, 1)

    for side in range(2):
        relay(ends[1], side).wait_recv()
    prepare(count - 1, True, (1,))
    work_last(pairs - 5, 0)

    def sent(step):
        for side in range(2):
            direct(step, side).wait_send()
            relay(step, side).wait_send()

    for step in tuple(range(early)) + ends:
        sent(step)

    @pl.loop(early, count - 1)
    def _(step):
        sent(step)

    for up in (True, False):
        for item in range(10):
            rim(up, item).wait_send()


def region_shards(states, weights, obs_count, neighbours):
    part, local_rows = states.shape
    members = part * lax.axis_size("member")
    count = local_rows // CHUNK
    pairs = local_rows // BLOCK
    blocks = pairs + 2 * REACH
    tiles, listed = neighbours.shape
    vmem = pl.BlockSpec(memory_space=pltpu.VMEM)
    anywhere = pl.BlockSpec(memory_space=pltpu.HBM)
    dma = pltpu.SemaphoreType.DMA
    bf16, f32 = jnp.bfloat16, jnp.float32
    operands = (states, weights, obs_count.reshape(1, tiles), neighbours.T)
    return pl.pallas_call(
        region_kernel,
        out_shape=jax.ShapeDtypeStruct((part, local_rows), f32),
        in_specs=[anywhere, anywhere, anywhere, anywhere],
        out_specs=vmem,
        scratch_shapes=[
            pltpu.VMEM((pairs, members, BLOCK), bf16),
            pltpu.VMEM((pairs, members, BLOCK), bf16),
            pltpu.VMEM((blocks, BLOCK, members), bf16),
            pltpu.VMEM((blocks, BLOCK, members), bf16),
            pltpu.VMEM((2 * part, blocks * BLOCK), bf16),
            pltpu.VMEM((SPAN, BLOCK, BLOCK), f32),
            pltpu.VMEM((2, 6 * BLOCK, BLOCK), bf16),
            pltpu.VMEM((2, 6 * BLOCK, BLOCK), bf16),
            pltpu.VMEM((4, 4 * BLOCK, BLOCK), bf16),
            pltpu.VMEM((4, 4 * BLOCK, BLOCK), bf16),
            pltpu.VMEM((count + 4, members, CHUNK), f32),
            pltpu.VMEM((part, local_rows), f32),
            pltpu.VMEM((2, part, RIM), f32),
            pltpu.VMEM((3, 1, tiles), jnp.int32),
            pltpu.VMEM((listed, tiles), jnp.int32),
            pltpu.VMEM((TILE, TILE), f32),
            pltpu.VMEM((tiles, TILE), f32),
            pltpu.VMEM((2 * HALO_TILES + 3, tiles, TILE), f32),
            dma((count,)), dma((3,)),
            dma((2, count + 1)), dma((2, count + 1)), dma((2, count + 1)), dma((2, count + 1)),
            dma((2, 10)), dma((2, 10)),
            pltpu.SemaphoreType.REGULAR, pltpu.SemaphoreType.REGULAR,
        ],
        compiler_params=pltpu.CompilerParams(
            collective_id=0, has_side_effects=True, vmem_limit_bytes=52 * 1024 * 1024
        ),
    )(*(pltpu.with_memory_space_constraint(value, pltpu.HBM) for value in operands))


def fits(states, weights, obs_count, neighbours):
    part, local_rows = states.shape
    members = part * lax.axis_size("member")
    window = local_rows + 2 * RIM
    return (
        lax.axis_size("member") == 4
        and lax.axis_size("region") > 2
        and local_rows % RIM == 0
        and 5 * RIM <= local_rows <= TILE * TILE
        and members == 256
        and window * (members * 12 + part * 16) <= 46 * 1024 * 1024
    )


def either(*arguments):
    return region_shards(*arguments) if fits(*arguments) else shards(*arguments)


def solution(mesh):
    placed = (P("member", "region"), P("member", "region"), P("region"), P("region", None))
    return jax.shard_map(
        either, mesh=mesh, in_specs=placed, out_specs=P("member", "region"), check_vma=False
    )
```

```python
import jax
import jax.numpy as jnp
from jax import lax
from jax.experimental import pallas as pl
from jax.experimental.pallas import tpu as pltpu
from jax.sharding import PartitionSpec as P

TILE = 128
HALO_TILES = 8
TPD = 12


def extended_2(block, sides, width):
    for axis, dim in sides:
        count = lax.axis_size(axis)
        forward = [(i, i + 1) for i in range(count - 1)]
        forward.append((count - 1, 0))
        backward = [(target, source) for source, target in forward]
        low = lax.ppermute(
            lax.slice_in_dim(block, block.shape[dim] - width, None, axis=dim), axis, forward
        )
        high = lax.ppermute(lax.slice_in_dim(block, 0, width, axis=dim), axis, backward)
        block = jnp.concatenate([low, block, high], axis=dim)
    return block


def taper(offset, tile):
    rows = jnp.arange(tile, dtype=jnp.float32)
    spread = tile * offset[:, None, None] + rows[None, None, :] - rows[None, :, None]
    scaled = spread / (2.0 * tile)
    return 1.0 / (1.0 + scaled * scaled)


def shards(states, weights, obs_count, neighbours):
    member_count = lax.axis_size("member")
    region_count = lax.axis_size("region")
    member_part, local_rows = states.shape
    local_tiles = local_rows // TILE
    counts = obs_count.astype(jnp.float32)
    factor = counts / (counts + 8.0)
    scaled = (weights.reshape(member_part, local_tiles, TILE) * factor[None, :, None]).reshape(
        member_part, local_rows
    )
    stacked = jnp.stack([states, scaled])
    rim = HALO_TILES * TILE
    block = TPD * TILE
    padded = extended_2(stacked, (("region", 2),), rim)
    own_block = lax.all_to_all(stacked, "member", split_axis=2, concat_axis=1, tiled=True)
    extended = extended_2(own_block, (("member", 2),), rim)
    below, above = (
        lax.all_gather(padded[:, :, :rim], "member", axis=1, tiled=True),
        lax.all_gather(padded[:, :, rim + local_rows :], "member", axis=1, tiled=True),
    )
    position = lax.axis_index("member")
    lower = jnp.where(position == 0, below, extended[:, :, :rim])
    upper = jnp.where(position == member_count - 1, above, extended[:, :, rim + block :])
    window = jnp.concatenate([lower, extended[:, :, rim : rim + block], upper], axis=2)
    members = window.shape[1]
    anomaly = window[0] - jnp.mean(window[0], axis=0, keepdims=True)
    window_weights = window[1]
    tiles_all = TPD * member_count * region_count
    first_tile = (lax.axis_index("region") * member_count + lax.axis_index("member")) * TPD
    lists = lax.dynamic_slice_in_dim(neighbours, lax.axis_index("member") * TPD, TPD, 0)
    local_ids = (lists - first_tile + HALO_TILES) % tiles_all
    span_count = 2 * HALO_TILES + 1
    tile_places = jnp.arange(TPD, dtype=jnp.int32)
    shift_places = jnp.arange(span_count, dtype=jnp.int32)
    wanted = tile_places[:, None, None] + shift_places[None, None, :]
    keep_table = jnp.sum((local_ids[:, :, None] == wanted).astype(jnp.float32), axis=1)
    mine = anomaly[:, rim : rim + block].reshape(members, TPD, TILE)

    def add_offset(shift, total):
        others = lax.dynamic_slice_in_dim(anomaly, shift * TILE, block, 1).reshape(
            members, TPD, TILE
        )
        other_weights = lax.dynamic_slice_in_dim(window_weights, shift * TILE, block, 1).reshape(
            members, TPD, TILE
        )
        covar = jnp.einsum("mti,mtj->tij", mine, others, precision=lax.Precision.HIGHEST) / (
            members - 1.0
        )
        offset = jnp.full((TPD,), shift - HALO_TILES).astype(jnp.float32)
        keep = lax.dynamic_index_in_dim(keep_table, shift, 1, keepdims=False)
        coefficient = taper(offset, TILE) * covar * keep[:, None, None]
        return total + jnp.einsum(
            "mtj,tij->mti", other_weights, coefficient, precision=lax.Precision.HIGHEST
        )

    total = lax.fori_loop(0, span_count, add_offset, jnp.zeros((members, TPD, TILE), jnp.float32))
    returned = lax.all_to_all(
        total.reshape(members, block), "member", split_axis=0, concat_axis=1, tiled=True
    )
    return returned


BLOCK = 2 * TILE
SPAN = HALO_TILES + 1
RIM = HALO_TILES * TILE
CHUNK = RIM // 2
REACH = HALO_TILES // 2


def split(value):
    high = value.astype(jnp.bfloat16)
    return high, (value - high.astype(jnp.float32)).astype(jnp.bfloat16)


def dot(left, right):
    return jnp.dot(left, right, preferred_element_type=jnp.float32)


def fill_taper(taper_ref, members):
    rows = lax.broadcasted_iota(jnp.int32, (BLOCK, BLOCK), 0)
    columns = lax.broadcasted_iota(jnp.int32, (BLOCK, BLOCK), 1)
    for k in range(SPAN):
        spread = (rows - columns + (2 * k - HALO_TILES) * TILE).astype(jnp.float32) / (2.0 * TILE)
        taper_ref[k] = 1.0 / ((1.0 + spread * spread) * (members - 1.0))


def region_kernel(
    own_ref, weights_ref, count_ref, lists_ref, out_ref,
    low_ref, high_ref, low_t_ref, high_t_ref, pair_ref, taper_ref, xh_a, xl_a, xh_b, xl_b,
    held, weight_held, weight_rim, counts_held, lists_held, turn_ref, factor_ref, keep_ref,
    own_sem, weight_sem, direct_send, direct_recv, relay_send, relay_recv, rim_send, rim_recv, up_sem, down_sem,
):
    part, rows = own_ref.shape
    count = rows // CHUNK
    half = part // 2
    pairs = rows // BLOCK
    tiles = rows // TILE
    rim_tiles = RIM // TILE
    member, region = lax.axis_index("member"), lax.axis_index("region")
    regions = lax.axis_size("region")
    beside = member + 1 - 2 * lax.rem(member, 2)
    across = lax.rem(member + 2, 4)
    partners = ((beside, region), (across, region))
    above = (member, lax.rem(region + 1, regions))
    below = (member, lax.rem(region + regions - 1, regions))
    order = (0, count - 1, 1, count - 2)
    early = len(order)

    first, last = region == 0, region == regions - 1

    def signal(semaphore, device):
        pl.semaphore_signal(semaphore, inc=1, device_id=device, device_id_type=pl.DeviceIdType.MESH)

    barrier = pltpu.get_barrier_semaphore()
    for device in partners:
        signal(barrier, device)

    @pl.when(jnp.logical_not(last))
    def _():
        signal(barrier, above)

    @pl.when(jnp.logical_not(first))
    def _():
        signal(barrier, below)

    @pl.when(first | last)
    def _():
        pl.semaphore_wait(barrier, 3)

    @pl.when(jnp.logical_not(first | last))
    def _():
        pl.semaphore_wait(barrier, 4)

    def chunk_at(step):
        return order[step] if isinstance(step, int) and step < early else step - 2

    def copy(source, target, send, recv, device):
        return pltpu.make_async_remote_copy(
            src_ref=source, dst_ref=target, send_sem=send, recv_sem=recv,
            device_id=device, device_id_type=pl.DeviceIdType.MESH,
        )

    def columns_of(chunk):
        return pl.ds(pl.multiple_of(chunk * CHUNK, CHUNK), CHUNK)

    def piece(step):
        if isinstance(step, int) and step >= count - 1:
            inner = pl.ds((step - count + 1) * BLOCK, BLOCK)
            return count - 3, inner, pl.ds((count - 3) * CHUNK + (step - count + 1) * BLOCK, BLOCK)
        chunk = chunk_at(step)
        return chunk, slice(None), columns_of(chunk)

    def strip(slot):
        return pl.ds(slot * part, part)

    def own_copy(chunk):
        return pltpu.make_async_copy(
            own_ref.at[:, columns_of(chunk)], held.at[chunk + 2, strip(0)], own_sem.at[chunk]
        )

    def direct(step, side):
        chunk, inner, columns = piece(step)
        return copy(
            own_ref.at[:, columns], held.at[chunk + 2, strip(1 + side), inner],
            direct_send.at[side, step], direct_recv.at[side, step], partners[side],
        )

    def relay(step, side):
        chunk, inner, _ = piece(step)
        source, target = pl.ds((2 - side) * part + side * half, half), pl.ds(3 * part + side * half, half)
        return copy(
            held.at[chunk + 2, source, inner], held.at[chunk + 2, target, inner],
            relay_send.at[side, step], relay_recv.at[side, step], partners[side],
        )

    def rim(up, item):
        device = above if up else below
        spot = 0 if up else 1
        if item >= 8:
            edge = slice(rows - RIM, rows) if up else slice(0, RIM)
            if item == 8:
                source, target = weights_ref.at[:, edge], weight_rim.at[spot]
            else:
                source, target = count_ref, counts_held.at[1 + spot]
        else:
            slot, edge = item // 2, item % 2
            chunk, place = (count - 2 + edge, edge) if up else (edge, count + 2 + edge)
            source = held.at[chunk + 2, strip(slot)] if slot else own_ref.at[:, columns_of(chunk)]
            target = held.at[place, strip(slot)]
        return copy(source, target, rim_send.at[spot, item], rim_recv.at[spot, item], device)

    def rim_of(step, slot):
        chunk = order[step]
        up = chunk >= count - 2
        return rim(up, 2 * slot + (chunk - count + 2 if up else chunk))

    for step in range(3):
        for side in range(2):
            direct(step, side).start()
    count_copy = pltpu.make_async_copy(count_ref, counts_held.at[0], weight_sem.at[1])
    lists_copy = pltpu.make_async_copy(lists_ref, lists_held, weight_sem.at[2])
    weight_copy = pltpu.make_async_copy(weights_ref, weight_held, weight_sem.at[0])
    count_copy.start()
    lists_copy.start()
    weight_copy.start()
    for chunk in range(count):
        own_copy(chunk).start()

    fill_taper(taper_ref, part * 4)
    turn_ref[...] = jnp.zeros_like(turn_ref)

    @pl.when(first)
    def _():
        signal(up_sem, above)

    @pl.when(last)
    def _():
        signal(down_sem, below)
        pl.semaphore_wait(up_sem, 1)

    @pl.when(jnp.logical_not(first | last))
    def _():
        pl.semaphore_wait(up_sem, 1)
        signal(up_sem, above)

    @pl.when((region > 1) & jnp.logical_not(last))
    def _():
        pl.semaphore_wait(down_sem, 1)
        signal(down_sem, below)

    at_once = (0, 1, 9, 8)
    for item in at_once:
        rim(True, item).start()

    @pl.when(jnp.logical_not(first))
    def _():
        for item in at_once:
            rim(False, item).start()

    def late_start():
        @pl.when(region == 1)
        def _():
            pl.semaphore_wait(down_sem, 1)
            signal(down_sem, below)

        @pl.when(first)
        def _():
            pl.semaphore_wait(down_sem, 1)
            for item in at_once:
                rim(False, item).start()
            for slot in range(1, 4):
                rim_of(0, slot).start()

    def pass_on(step, slots):
        def start():
            for slot in slots:
                rim_of(step, slot).start()

        if step == 0:
            pl.when(jnp.logical_not(first))(start)
        else:
            start()

    def prepare_weights(value, columns):
        high, low = split(value)
        pair_ref[0:part, columns] = high
        pair_ref[part : 2 * part, columns] = low

    def factors_of(which):
        turn_ref[0:1, 0:tiles] = counts_held[which].astype(jnp.float32)
        spread = jnp.broadcast_to(turn_ref[...].T[0:tiles, 0:1], (tiles, TILE))
        return spread / (spread + 8.0)

    count_copy.wait()
    factor_ref[...] = factors_of(0)
    lists_copy.wait()
    tiles_all = regions * tiles
    own_tile = region * tiles + lax.broadcasted_iota(jnp.int32, lists_held.shape, 1)
    shift = lists_held[...] - own_tile + HALO_TILES
    shift = jnp.where(shift < 0, shift + tiles_all, jnp.where(shift >= tiles_all, shift - tiles_all, shift))
    turn_ref[0 : shift.shape[0], 0:tiles] = shift.astype(jnp.float32)
    turned = turn_ref[...].T
    spreads = [jnp.broadcast_to(turned[0:tiles, i : i + 1], (tiles, TILE)) for i in range(shift.shape[0])]
    for place in range(2 * HALO_TILES + 3):
        total = jnp.zeros((tiles, TILE), jnp.float32)
        for spread in spreads:
            total = total + jnp.where(spread == place - 1.0, 1.0, 0.0)
        keep_ref[place] = total

    weight_copy.wait()

    @pl.loop(0, pairs)
    def _(block):
        for t in range(2):
            start = block * BLOCK + t * TILE
            columns = pl.ds(pl.multiple_of(start, TILE), TILE)
            target = pl.ds(pl.multiple_of(start + RIM, TILE), TILE)
            prepare_weights(weight_held[:, columns] * factor_ref[pl.ds(2 * block + t, 1)], target)

    def prepare(place, own, parts=(0, 1)):
        for b in parts:
            value = held[place, :, b * BLOCK : (b + 1) * BLOCK]
            anomaly = value - jnp.mean(value, axis=0, keepdims=True)
            block = place * (CHUNK // BLOCK) + b
            high_t_ref[block], low_t_ref[block] = split(anomaly.T)
            if own:
                high_ref[block - REACH], low_ref[block - REACH] = split(anomaly)

    def put(scaled, pair, k, held_x, buffer, spot):
        xh_ref, xl_ref = held_x
        for t in range(2):
            for s in range(2):
                inner, outer = slice(t * TILE, (t + 1) * TILE), slice(s * TILE, (s + 1) * TILE)
                value = scaled[inner, outer] * keep_ref[2 * k + t + 1 - s, pl.ds(2 * pair + s, 1)]
                place = slice(spot * BLOCK + t * TILE, spot * BLOCK + (t + 1) * TILE)
                xh_ref[buffer, place, outer], xl_ref[buffer, place, outer] = split(value)

    def cross(pair, k, place, mirror=None):
        left_high, left_low = high_t_ref[pair + k], low_t_ref[pair + k]
        right_high, right_low = high_ref[pair], low_ref[pair]
        covar = dot(left_high, right_high) + dot(left_low, right_high) + dot(left_high, right_low)
        scaled = covar * taper_ref[k]
        put(scaled, pair, k, *place)
        if mirror is not None:
            put(scaled.T, pair + k - REACH, 2 * REACH - k, *mirror)

    def apply(pair, k, length, held_x, buffer, fresh, spot=0):
        xh_ref, xl_ref = held_x
        columns = pl.ds(pl.multiple_of((pair + k) * BLOCK, BLOCK), length * BLOCK)
        place = slice(spot * BLOCK, (spot + length) * BLOCK)
        both = dot(pair_ref[:, columns], xh_ref[buffer, place])
        term = both[:part] + both[part:] + dot(pair_ref[0:part, columns], xl_ref[buffer, place])
        target = pl.ds(pl.multiple_of(pair * BLOCK, BLOCK), BLOCK)
        out_ref[:, target] = term if fresh else out_ref[:, target] + term

    wide, narrow = (xh_a, xl_a), (xh_b, xl_b)

    def work_edge(base):
        for i in range(4):
            for j in range(i):
                cross(base + i, REACH + j - i, (narrow, i, j), (narrow, j, i))
            cross(base + i, REACH, (narrow, i, i))
        for i in range(4):
            apply(base + i, REACH - i, 4, narrow, i, True)

    def work_inner(chunk):
        base = 2 * chunk
        for i in range(4):
            cross(base, i, (wide, 0, i), (narrow, i, 0))
        cross(base, 4, (wide, 0, 4))
        cross(base, 5, (wide, 0, 5), (wide, 1, 3))
        for i in range(3):
            cross(base + 1, i, (wide, 1, i), (narrow, i + 1, 1))
        cross(base + 1, 4, (wide, 1, 4))
        apply(base, 0, 6, wide, 0, True)
        apply(base + 1, 0, 5, wide, 1, True)
        for i in range(4):
            apply(base - 4 + i, 8 - i, min(i + 1, 2), narrow, i, False)

    def work_close():
        base = pairs - 8
        cross(base, 8, (narrow, 0, 0), (narrow, 2, 0))
        cross(base + 1, 7, (narrow, 1, 0), (narrow, 2, 1))
        cross(base + 1, 8, (narrow, 1, 1), (narrow, 3, 0))
        apply(base, 8, 1, narrow, 0, False)
        apply(base + 1, 7, 2, narrow, 1, False)
        apply(base + 4, 0, 2, narrow, 2, False)
        apply(base + 5, 0, 1, narrow, 3, False)

    def work_last(base, gap):
        above_ks = range(REACH + 1 + gap, 2 * REACH + 1)
        for i in range(REACH):
            cross(base, i, (wide, 0, i), (narrow, i, 0))
        cross(base, REACH, (wide, 0, REACH))
        for i, k in enumerate(above_ks):
            cross(base, k, (wide, 1, i), (narrow, i, 1))
        apply(base, 0, REACH + 1, wide, 0, True)
        apply(base, above_ks[0], len(above_ks), wide, 1, False)
        for i in range(REACH):
            apply(base - REACH + i, 2 * REACH - i, 1, narrow, i, False)
        for i, k in enumerate(above_ks):
            apply(base + k - REACH, 2 * REACH - k, 1, narrow, i, False, 1)

    def work_rim(up):
        place = count + 2 if up else 0
        spot = 1 if up else 0
        for item in range(10):
            rim(not up, item).wait_recv()

        @pl.loop(0, 2)
        def _(edge):
            prepare(place + edge, False)

        factors = factors_of(1 + spot)
        for t in range(rim_tiles):
            inner = slice(t * TILE, (t + 1) * TILE)
            start = (rows + RIM if up else 0) + t * TILE
            tile = t if up else tiles - rim_tiles + t
            prepare_weights(weight_rim[spot, :, inner] * factors[tile : tile + 1], slice(start, start + TILE))
        for i in range(4):
            pair, first_k, length = (pairs - 4 + i, 8 - i, i + 1) if up else (i, 0, 4 - i)
            for spot in range(length):
                cross(pair, first_k + spot, (narrow, i, spot))
        for i in range(4):
            pair, first_k, length = (pairs - 4 + i, 8 - i, i + 1) if up else (i, 0, 4 - i)
            apply(pair, first_k, length, narrow, i, False)

    def forward(step):
        for side in range(2):
            direct(step, side).wait_recv()
        for side in range(2):
            relay(step, side).start()
        if isinstance(step, int) and step < early:
            pass_on(step, (1, 2))

    for chunk in range(count):
        own_copy(chunk).wait()
    forward(0)

    for step in range(early):
        forward(step + 1)
        for side in range(2):
            direct(step + 3, side).start()
        for side in range(2):
            relay(step, side).wait_recv()
        pass_on(step, (3,))
        prepare(order[step] + 2, True)
        if step == 0:
            late_start()
        if step >= 2:
            work_edge(0 if step == 2 else pairs - 4)

    ends = (count - 1, count)

    @pl.loop(early, count - 1)
    def _(step):
        @pl.when(step + 1 < count - 1)
        def _():
            forward(step + 1)

        @pl.when(step + 3 < count - 1)
        def _():
            for side in range(2):
                direct(step + 3, side).start()

        for end in ends:
            @pl.when(step + 3 == end)
            def _():
                for side in range(2):
                    direct(end, side).start()

            @pl.when(step + 1 == end)
            def _():
                forward(end)

        for side in range(2):
            relay(step, side).wait_recv()
        chunk = chunk_at(step)
        prepare(chunk + 2, True)
        work_inner(chunk)

        @pl.when(chunk == 4)
        def _():
            work_rim(False)

        @pl.when(chunk == 5)
        def _():
            work_rim(True)

        @pl.when(chunk == count - 4)
        def _():
            forward(ends[1])
            work_close()

    for side in range(2):
        relay(ends[0], side).wait_recv()
    prepare(count - 1, True, (0,))
    work_last(pairs - 6, 1)

    for side in range(2):
        relay(ends[1], side).wait_recv()
    prepare(count - 1, True, (1,))
    work_last(pairs - 5, 0)

    def sent(step):
        for side in range(2):
            direct(step, side).wait_send()
            relay(step, side).wait_send()

    for step in tuple(range(early)) + ends:
        sent(step)

    @pl.loop(early, count - 1)
    def _(step):
        sent(step)

    for up in (True, False):
        for item in range(10):
            rim(up, item).wait_send()


def region_shards(states, weights, obs_count, neighbours):
    part, local_rows = states.shape
    members = part * lax.axis_size("member")
    count = local_rows // CHUNK
    pairs = local_rows // BLOCK
    blocks = pairs + 2 * REACH
    tiles, listed = neighbours.shape
    vmem = pl.BlockSpec(memory_space=pltpu.VMEM)
    anywhere = pl.BlockSpec(memory_space=pltpu.HBM)
    dma = pltpu.SemaphoreType.DMA
    bf16, f32 = jnp.bfloat16, jnp.float32
    operands = (states, weights, obs_count.reshape(1, tiles), neighbours.T)
    return pl.pallas_call(
        region_kernel,
        out_shape=jax.ShapeDtypeStruct((part, local_rows), f32),
        in_specs=[anywhere, anywhere, anywhere, anywhere],
        out_specs=vmem,
        scratch_shapes=[
            pltpu.VMEM((pairs, members, BLOCK), bf16),
            pltpu.VMEM((pairs, members, BLOCK), bf16),
            pltpu.VMEM((blocks, BLOCK, members), bf16),
            pltpu.VMEM((blocks, BLOCK, members), bf16),
            pltpu.VMEM((2 * part, blocks * BLOCK), bf16),
            pltpu.VMEM((SPAN, BLOCK, BLOCK), f32),
            pltpu.VMEM((2, 6 * BLOCK, BLOCK), bf16),
            pltpu.VMEM((2, 6 * BLOCK, BLOCK), bf16),
            pltpu.VMEM((4, 4 * BLOCK, BLOCK), bf16),
            pltpu.VMEM((4, 4 * BLOCK, BLOCK), bf16),
            pltpu.VMEM((count + 4, members, CHUNK), f32),
            pltpu.VMEM((part, local_rows), f32),
            pltpu.VMEM((2, part, RIM), f32),
            pltpu.VMEM((3, 1, tiles), jnp.int32),
            pltpu.VMEM((listed, tiles), jnp.int32),
            pltpu.VMEM((TILE, TILE), f32),
            pltpu.VMEM((tiles, TILE), f32),
            pltpu.VMEM((2 * HALO_TILES + 3, tiles, TILE), f32),
            dma((count,)), dma((3,)),
            dma((2, count + 1)), dma((2, count + 1)), dma((2, count + 1)), dma((2, count + 1)),
            dma((2, 10)), dma((2, 10)),
            pltpu.SemaphoreType.REGULAR, pltpu.SemaphoreType.REGULAR,
        ],
        compiler_params=pltpu.CompilerParams(
            collective_id=0, has_side_effects=True, vmem_limit_bytes=52 * 1024 * 1024
        ),
    )(*(pltpu.with_memory_space_constraint(value, pltpu.HBM) for value in operands))


def fits(states, weights, obs_count, neighbours):
    part, local_rows = states.shape
    members = part * lax.axis_size("member")
    window = local_rows + 2 * RIM
    return (
        lax.axis_size("member") == 4
        and lax.axis_size("region") > 2
        and local_rows % RIM == 0
        and 5 * RIM <= local_rows <= TILE * TILE
        and members == 256
        and window * (members * 12 + part * 16) <= 46 * 1024 * 1024
    )


def either(*arguments):
    return region_shards(*arguments) if fits(*arguments) else shards(*arguments)


def solution(mesh):
    placed = (P("member", "region"), P("member", "region"), P("region"), P("region", None))
    return jax.shard_map(
        either, mesh=mesh, in_specs=placed, out_specs=P("member", "region"), check_vma=False
    )
```
